32 devices in a mesh: dp: 8 (over z, y), tensor: 4 (over x, core).
Axes of the slice: x: 2, y: 2, z: 4, core: 2. Of those that a mesh axis runs over, the one named last changes fastest.
Arguments:
- activations: bfloat16 [2048, 8192], P('dp'), may hold values from -6 to 6
- key_value_grads: bfloat16 [2048, 2, 1024], P('dp', None, 'tensor'), may hold values from -6 to 6
- owner_table: int32 [64], replicated, may hold values from 0 to 63, each once
- left_factors: float32 [4, 64, 512, 512], P('tensor', 'dp'), may hold values from -16 to 16, as said below
- right_factors: float32 [4, 64, 128, 128], P('tensor', 'dp'), may hold values from -16 to 16, as said below
Outputs:
- left_updated: float32 [4, 64, 512, 512], P('tensor', 'dp')
- right_updated: float32 [4, 64, 128, 128], P('tensor', 'dp')
- update: bfloat16 [2, 8192, 1024], P(None, 'dp')
The draws below stay inside these ranges and needn't reach their ends.
Inputs may be any that keep to these rules, and one draw needn't show every extreme that they name: `owner_table`: each block number appears once; slot s lies on index s // 8 of dp. `left_factors`: every block is symmetric positive definite. `right_factors`: every block is symmetric positive definite.
All inputs are finite; a program needn't handle non-finite values.
Results may differ from the reference program's by a relative error of at most 0.012.
The reference program's roundings to bfloat16 on the way (of `direction`) count: a program that leaves them out, or rounds other values in their place, can miss the bound.
Values may be sent and summed in bfloat16 or wider, within the bound.
A program may use at most 128 MiB of HBM per device.

```python
import jax
import jax.numpy as jnp
from jax import lax

D = 8192
KVW = 1024
BC = 128
BL = 512
ITERS = 8
TOKENS = 2048
TSH = 4
CB = 2
NRB = 16
NBLK = 64


def factor_draw(base_key, salt_value, order_dim, scale_value):
    mixed_key = jax.random.fold_in(base_key, salt_value)
    first_key = jax.random.fold_in(mixed_key, 0)
    base_draw = jax.random.normal(first_key, (TSH, NBLK, order_dim, order_dim), jnp.float32)
    wishart = jnp.einsum('tsik,tsjk->tsij', base_draw, base_draw) / order_dim
    shaped = wishart + 0.25 * jnp.eye(order_dim, dtype=jnp.float32)
    return shaped * scale_value


def draw_left_factors(key, part):
    return factor_draw(key, 11, BL, BC / TOKENS)


def draw_right_factors(key, part):
    return factor_draw(key, 23, BC, BL / TOKENS)


def with_spikes(values, rng, source, target, shards_of, factor):
    def block_of(position):
        return (jnp.arange(values.shape[position]) // (values.shape[position] // shards_of)).reshape((-1,) + (1,) * (values.ndim - 1 - position))

    first = jax.random.permutation(rng, shards_of)[block_of(target)]
    far = (block_of(target) + shards_of // 2) % shards_of
    return jnp.where((block_of(source) == first) | (block_of(source) == far), factor * values, values)


def block_scale(key, dims, shards, low, high):
    def one(position, shards_of):
        steps = jax.random.uniform(jax.random.fold_in(jax.random.fold_in(key, 6), position), (shards_of,), jnp.float32, low / len(shards), high / len(shards))
        return jnp.repeat(jnp.exp(steps), dims[position] // shards_of).reshape((-1,) + (1,) * (len(dims) - position - 1))

    gain = one(*shards[0])
    for cut in shards[1:]:
        gain = gain * one(*cut)
    return gain


def centred(key, extent, width, limit, pieces=(), kind=jnp.bfloat16):
    entries = jax.random.normal(key, extent, jnp.float32) * width
    if len(pieces) > 0:
        entries = block_scale(key, extent, pieces, -0.22, 0.18) * entries
    return jnp.clip(entries, min=-limit, max=limit).astype(kind)


def heavy_noise(rng, dims, scale, reach, cuts, heavy, held_as=jnp.bfloat16):
    values = scale * jax.random.normal(rng, dims, jnp.float32)
    if cuts:
        values = values * block_scale(rng, dims, cuts, -0.22, 0.18)
    return jnp.clip(with_spikes(values, jax.random.fold_in(rng, 3), *heavy), -reach, reach).astype(held_as)


def setup_inputs(seed: int = 0) -> dict:
    arg_keys = jax.random.split(jax.random.key(seed), 6)
    activations = heavy_noise(arg_keys[0], (TOKENS, D), 1.0, 6.0, ((0, 8),), (0, 1, 8, 2.0))
    key_value_grads = centred(arg_keys[1], (TOKENS, 2, KVW), 1.0, 6.0, ((0, 8), (2, 4)))
    owner_table = jax.random.permutation(arg_keys[2], NBLK).astype(jnp.int32)
    left_factors = draw_left_factors(jax.random.fold_in(arg_keys[5], 71), 0)
    right_factors = draw_right_factors(jax.random.fold_in(arg_keys[5], 71), 0)
    return dict(activations=activations, key_value_grads=key_value_grads, owner_table=owner_table, left_factors=left_factors, right_factors=right_factors)


MOMENT_DECAY = 0.9
RIDGE_SHARE = 0.0001
EXACT_MODE = lax.Precision.HIGHEST

def product(left_mat, right_mat):
    return jnp.dot(left_mat, right_mat, precision=EXACT_MODE, preferred_element_type=jnp.float32)

def rounded(matrix):
    narrow = lax.optimization_barrier(matrix.astype(jnp.bfloat16))
    return narrow.astype(jnp.float32)

def coarse_product(left_mat, right_mat):
    return product(rounded(left_mat), rounded(right_mat))

def inverse_root(matrix):
    order_dim = matrix.shape[0]
    identity_mat = jnp.eye(order_dim, dtype=jnp.float32)
    shifted = matrix + RIDGE_SHARE * jnp.trace(matrix) / order_dim * identity_mat
    scaling = 2.5 / jnp.sqrt(jnp.sum(shifted * shifted))
    result = jnp.sqrt(jnp.sqrt(scaling)) * identity_mat
    powered = scaling * shifted
    for iteration in range(ITERS):
        factor = (5.0 * identity_mat - powered) * 0.25
        result = coarse_product(result, factor)
        if iteration + 1 < ITERS:
            squared = coarse_product(factor, factor)
            powered = coarse_product(coarse_product(squared, squared), powered)
    return result

def block_step(inputs):
    gradient, left_old, right_old = inputs
    left_new = MOMENT_DECAY * left_old + (1.0 - MOMENT_DECAY) * product(gradient, gradient.T)
    right_new = MOMENT_DECAY * right_old + (1.0 - MOMENT_DECAY) * product(gradient.T, gradient)
    precond = product(product(inverse_root(left_new), gradient), inverse_root(right_new))
    direction = precond / jnp.sqrt(jnp.mean(precond * precond) + 1e-06)
    return (left_new, right_new, direction.astype(jnp.bfloat16))

def reference(activations, key_value_grads, owner_table, left_factors, right_factors):
    sums = []
    for which in range(2):
        sums.append(jnp.dot(activations.T, key_value_grads[:, which, :], preferred_element_type=jnp.float32) / TOKENS)
    full_grad = jnp.stack(sums)
    canonical = full_grad.reshape(2, NRB, BL, TSH, CB, BC).transpose(3, 0, 1, 4, 2, 5).reshape(TSH, NBLK, BL, BC)
    by_slot = jnp.take(canonical, owner_table, axis=1)
    left_new, right_new, directions = lax.map(block_step, (by_slot.reshape(TSH * NBLK, BL, BC), left_factors.reshape(TSH * NBLK, BL, BL), right_factors.reshape(TSH * NBLK, BC, BC)))
    directions = directions.reshape(TSH, NBLK, BL, BC)
    placed = jnp.zeros((TSH, NBLK, BL, BC), jnp.bfloat16).at[:, owner_table].set(directions)
    update = placed.reshape(TSH, 2, NRB, CB, BL, BC).transpose(1, 2, 4, 0, 3, 5).reshape(2, D, KVW)
    return (left_new.reshape(TSH, NBLK, BL, BL), right_new.reshape(TSH, NBLK, BC, BC), update)
```

```python
import functools

import jax
import jax.numpy as jnp
from jax import lax
from jax.experimental import pallas as pl
from jax.experimental.pallas import tpu as pltpu
from jax.sharding import PartitionSpec as P

ITERS = 8
MOMENT_DECAY = 0.9
RIDGE_SHARE = 0.0001
CHUNK_SLOTS = 2
VMEM_LIMIT = 60 * 1024 * 1024


def dot(left_mat, right_mat):
    return jnp.dot(left_mat, right_mat, preferred_element_type=jnp.float32)


def halves(x):
    high = x.astype(jnp.bfloat16)
    low = (x - high.astype(jnp.float32)).astype(jnp.bfloat16)
    return high, low


def gradient_kernel(
    table_ref, act_ref, kv_ref, out_ref, *, chunk, chunk_slots, slots, per_projection, col_blocks, scale
):
    rows_block, cols_block = out_ref.shape[2:]
    width = col_blocks * cols_block
    first = pl.program_id(0) * slots + chunk * chunk_slots
    for k in range(chunk_slots):
        block_id = table_ref[first + k]
        projection = block_id // per_projection
        remainder = block_id % per_projection
        row_start = pl.multiple_of(remainder // col_blocks * rows_block, rows_block)
        col_start = pl.multiple_of(
            projection * width + remainder % col_blocks * cols_block, cols_block
        )
        summed = lax.dot_general(
            act_ref[:, pl.ds(row_start, rows_block)],
            kv_ref[:, pl.ds(col_start, cols_block)],
            (((0,), (0,)), ((), ())),
            preferred_element_type=jnp.float32,
        )
        out_ref[0, k] = summed * scale


def gradient_chunk(table, activations, cotangents, chunk, chunk_slots, ranks, rows_block, cols_block, col_blocks):
    tokens, model = activations.shape
    slots = table.shape[0] // ranks
    body = functools.partial(
        gradient_kernel,
        chunk=chunk,
        chunk_slots=chunk_slots,
        slots=slots,
        per_projection=model // rows_block * col_blocks,
        col_blocks=col_blocks,
        scale=1.0 / (tokens * ranks),
    )
    return pl.pallas_call(
        body,
        out_shape=jax.ShapeDtypeStruct((ranks, chunk_slots, rows_block, cols_block), jnp.float32),
        grid_spec=pltpu.PrefetchScalarGridSpec(
            num_scalar_prefetch=1,
            grid=(ranks,),
            in_specs=[
                pl.BlockSpec(activations.shape, lambda d, t: (0, 0), pipeline_mode=pl.Buffered(1)),
                pl.BlockSpec(cotangents.shape, lambda d, t: (0, 0), pipeline_mode=pl.Buffered(1)),
            ],
            out_specs=pl.BlockSpec(
                (1, chunk_slots, rows_block, cols_block), lambda d, t: (d, 0, 0, 0)
            ),
        ),
        compiler_params=pltpu.CompilerParams(vmem_limit_bytes=VMEM_LIMIT),
        cost_estimate=pl.CostEstimate(
            flops=2 * ranks * chunk_slots * rows_block * cols_block * tokens,
            bytes_accessed=activations.size * 2 + ranks * chunk_slots * rows_block * cols_block * 4,
            transcendentals=0,
        ),
    )(table, activations, cotangents)


def diagonal(order):
    rows = lax.broadcasted_iota(jnp.int32, (order, order), 0)
    return rows == lax.broadcasted_iota(jnp.int32, (order, order), 1)


def total(x):
    return jnp.sum(jnp.sum(x, axis=1, keepdims=True), axis=0, keepdims=True)


def factor_of(powered, on_diagonal):
    return ((jnp.where(on_diagonal, 5.0, 0.0) - powered) * 0.25).astype(jnp.bfloat16)


def begin_root(updated, m_ref, f_ref, x_ref):
    order = updated.shape[0]
    on_diagonal = diagonal(order)
    trace = total(jnp.where(on_diagonal, updated, 0.0))
    shifted = updated + jnp.where(on_diagonal, RIDGE_SHARE * trace / order, 0.0)
    scaling = 2.5 / jnp.sqrt(total(shifted * shifted))
    powered = scaling * shifted
    factor = factor_of(powered, on_diagonal)
    start = jnp.sqrt(jnp.sqrt(scaling)).astype(jnp.bfloat16).astype(jnp.float32)
    m_ref[...] = powered.astype(jnp.bfloat16)
    f_ref[...] = factor
    x_ref[...] = start * factor.astype(jnp.float32)


def root_steps(groups):
    squares = []
    for m_ref, f_ref, x_ref in groups:
        factor = f_ref[...]
        squares.append(dot(factor, factor).astype(jnp.bfloat16))
    fourths = [dot(s, s).astype(jnp.bfloat16) for s in squares]
    for fourth, (m_ref, f_ref, x_ref) in zip(fourths, groups):
        powered = dot(fourth, m_ref[...])
        m_ref[...] = powered.astype(jnp.bfloat16)
        f_ref[...] = factor_of(powered, diagonal(powered.shape[0]))
    for m_ref, f_ref, x_ref in groups:
        x_ref[...] = dot(x_ref[...].astype(jnp.bfloat16), f_ref[...])


def block_kernel(grad_ref, left_ref, right_ref, *rest, chunk_slots, chained):
    if chained:
        rest = rest[2:]
    left_out, right_out, dir_ref, ml, fl, xl, mr, fr, xr = rest
    groups = []
    for k in range(chunk_slots):
        grad = grad_ref[k]
        high, low = halves(grad)
        flipped = grad.T
        high_t, low_t = halves(flipped)
        wide = jnp.concatenate([high, high, low], axis=1)
        wide_t = jnp.concatenate([high_t, high_t, low_t], axis=1)
        tall = jnp.concatenate([high, low, high], axis=0)
        tall_t = jnp.concatenate([high_t, low_t, high_t], axis=0)
        left_new = MOMENT_DECAY * left_ref[k] + (1.0 - MOMENT_DECAY) * dot(wide, tall_t)
        right_new = MOMENT_DECAY * right_ref[k] + (1.0 - MOMENT_DECAY) * dot(wide_t, tall)
        left_out[k] = left_new
        right_out[k] = right_new
        begin_root(left_new, ml.at[k], fl.at[k], xl.at[k])
        begin_root(right_new, mr.at[k], fr.at[k], xr.at[k])
        groups.append((ml.at[k], fl.at[k], xl.at[k]))
        groups.append((mr.at[k], fr.at[k], xr.at[k]))

    def step(_, carry):
        root_steps(groups)
        return carry

    lax.fori_loop(0, ITERS - 1, step, 0)
    for k in range(chunk_slots):
        high, low = halves(grad_ref[k])
        tall = jnp.concatenate([high, low, high], axis=0)
        root_high, root_low = halves(xl[k])
        half = dot(jnp.concatenate([root_high, root_high, root_low], axis=1), tall)
        half_high, half_low = halves(half)
        right_high, right_low = halves(xr[k])
        precond = dot(
            jnp.concatenate([half_high, half_high, half_low], axis=1),
            jnp.concatenate([right_high, right_low, right_high], axis=0),
        )
        mean = total(precond * precond) / precond.size
        dir_ref[k] = (precond / jnp.sqrt(mean + 1e-06)).astype(jnp.bfloat16)


def block_chunk(grads, left_factors, right_factors, chunk, before):
    chunk_slots, rows_block, cols_block = grads.shape

    def pick(*tail):
        return pl.BlockSpec((chunk_slots,) + tail, lambda g: (chunk, 0, 0))

    def whole(*tail):
        return pl.BlockSpec((chunk_slots,) + tail, lambda g: (0, 0, 0))

    chained = before is not None
    specs = [
        whole(rows_block, cols_block),
        pick(rows_block, rows_block),
        pick(cols_block, cols_block),
    ]
    operands = [grads, left_factors, right_factors]
    aliases = {}
    if chained:
        specs += [pl.BlockSpec(memory_space=pl.ANY)] * 2
        operands += list(before)
        aliases = {3: 0, 4: 1}

    def scratch(order):
        square = (chunk_slots, order, order)
        return [
            pltpu.VMEM(square, jnp.bfloat16),
            pltpu.VMEM(square, jnp.bfloat16),
            pltpu.VMEM(square, jnp.float32),
        ]

    return pl.pallas_call(
        functools.partial(block_kernel, chunk_slots=chunk_slots, chained=chained),
        grid=(1,),
        out_shape=(
            jax.ShapeDtypeStruct(left_factors.shape, jnp.float32),
            jax.ShapeDtypeStruct(right_factors.shape, jnp.float32),
            jax.ShapeDtypeStruct(grads.shape, jnp.bfloat16),
        ),
        in_specs=specs,
        out_specs=(
            pick(rows_block, rows_block),
            pick(cols_block, cols_block),
            whole(rows_block, cols_block),
        ),
        scratch_shapes=scratch(rows_block) + scratch(cols_block),
        input_output_aliases=aliases,
        compiler_params=pltpu.CompilerParams(vmem_limit_bytes=VMEM_LIMIT),
        cost_estimate=pl.CostEstimate(
            flops=2 * chunk_slots * rows_block**3 * 4 * ITERS,
            bytes_accessed=chunk_slots * rows_block * rows_block * 8,
            transcendentals=0,
        ),
    )(*operands)


def pick_kernel(dev_ref, pos_ref, sub_ref, *refs, shape, chunk_slots, piece_rows, cols_block):
    sources, out_ref, sem = refs[:-2], refs[-2], refs[-1]
    projections, per_shard, col_blocks = shape
    index = 0
    for projection in range(projections):
        for piece in range(per_shard):
            for column in range(col_blocks):
                dest = out_ref.at[
                    projection,
                    pl.ds(piece * piece_rows, piece_rows),
                    pl.ds(column * cols_block, cols_block),
                ]
                rows = pl.ds(pl.multiple_of(sub_ref[piece] * piece_rows, piece_rows), piece_rows)
                for chunk, source in enumerate(sources):

                    @pl.when(pos_ref[index] // chunk_slots == chunk)
                    def _():
                        pltpu.make_async_copy(
                            source.at[dev_ref[index], pos_ref[index] % chunk_slots, rows], dest, sem.at[index]
                        ).start()

                index += 1
    index = 0
    for projection in range(projections):
        for piece in range(per_shard):
            for column in range(col_blocks):
                dest = out_ref.at[
                    projection,
                    pl.ds(piece * piece_rows, piece_rows),
                    pl.ds(column * cols_block, cols_block),
                ]
                pltpu.make_async_copy(
                    sources[0].at[0, 0, pl.ds(0, piece_rows)], dest, sem.at[index]
                ).wait()
                index += 1


def pick_rows(gathered, owner_table, shard_rows, row_blocks, col_blocks, slots):
    _, chunk_slots, block_order, cols_block = gathered[0].shape
    piece_rows = min(shard_rows, block_order)
    per_block = block_order // piece_rows
    per_shard = shard_rows // piece_rows
    pieces = lax.axis_index("dp") * per_shard + jnp.arange(per_shard, dtype=jnp.int32)
    wanted = (
        jnp.arange(2, dtype=jnp.int32)[:, None, None] * row_blocks + (pieces // per_block)[None, :, None]
    ) * col_blocks + jnp.arange(col_blocks, dtype=jnp.int32)[None, None, :]
    hits = wanted.reshape(-1)[:, None] == owner_table[None, :]
    where = jnp.sum(
        jnp.where(hits, jnp.arange(owner_table.shape[0], dtype=jnp.int32)[None, :], 0), axis=1, dtype=jnp.int32
    )
    count = 2 * per_shard * col_blocks
    body = functools.partial(
        pick_kernel,
        shape=(2, per_shard, col_blocks),
        chunk_slots=chunk_slots,
        piece_rows=piece_rows,
        cols_block=cols_block,
    )
    shape = (2, shard_rows, col_blocks * cols_block)
    return pl.pallas_call(
        body,
        out_shape=jax.ShapeDtypeStruct(shape, jnp.bfloat16),
        grid_spec=pltpu.PrefetchScalarGridSpec(
            num_scalar_prefetch=3,
            grid=(1,),
            in_specs=[pl.BlockSpec(memory_space=pl.ANY)] * len(gathered),
            out_specs=pl.BlockSpec(shape, lambda g, *_: (0, 0, 0)),
            scratch_shapes=[pltpu.SemaphoreType.DMA((count,))],
        ),
    )(where // slots, where % slots, pieces % per_block, *gathered)


def gathered_path(activations, key_value_grads, owner_table, left_factors, right_factors):
    rows_block = left_factors.shape[2]
    cols_block = right_factors.shape[2]
    ranks = lax.axis_size("dp")
    row_blocks = activations.shape[1] // rows_block
    col_blocks = key_value_grads.shape[2] // cols_block
    shard_rows = activations.shape[1] // ranks
    slots = left_factors.shape[1]
    chunk_slots = min(CHUNK_SLOTS, slots)
    cotangents = key_value_grads.reshape(key_value_grads.shape[0], -1)
    grads = []
    for chunk in range(slots // chunk_slots):
        partial = gradient_chunk(
            owner_table, activations, cotangents, chunk, chunk_slots, ranks, rows_block, cols_block, col_blocks
        )
        grads.append(lax.psum_scatter(partial, "dp", scatter_dimension=0, tiled=True)[0])
    before = None
    gathered = []
    for chunk, grad in enumerate(grads):
        left_new, right_new, directions = block_chunk(grad, left_factors[0], right_factors[0], chunk, before)
        before = (left_new, right_new)
        gathered.append(lax.all_gather(directions, "dp", axis=0))
    own_rows = pick_rows(gathered, owner_table, shard_rows, row_blocks, col_blocks, slots)
    update = lax.all_gather(own_rows, "tensor", axis=2, tiled=True)
    return (left_new[None], right_new[None], update)


def plan_kernel(table_ref, plan_ref, by_source, by_dest, free_source, free_dest, *, ranks, dest_of):
    def lowest(mask):
        found = 0
        for colour in reversed(range(ranks)):
            found = jnp.where((mask >> colour) & 1 == 1, colour, found)
        return found

    def clear(i, carry):
        by_source[i] = -1
        by_dest[i] = -1
        return carry

    lax.fori_loop(0, ranks * ranks, clear, 0)
    for i in range(ranks):
        free_source[i] = (1 << ranks) - 1
        free_dest[i] = (1 << ranks) - 1

    def place(slot, carry):
        source = slot // ranks
        dest = dest_of(table_ref[slot])
        both = free_source[source] & free_dest[dest]
        shared = both != 0
        first = lowest(jnp.where(shared, both, free_source[source]))
        second = lowest(jnp.where(shared, both, free_dest[dest]))
        moved = by_dest[dest * ranks + first]
        by_dest[dest * ranks + first] = slot
        by_source[source * ranks + first] = slot
        free_source[source] = free_source[source] & ~(1 << first)
        free_dest[dest] = free_dest[dest] & ~(1 << second)

        @pl.when(jnp.logical_not(shared))
        def _():
            by_dest[dest * ranks + second] = moved

        def swap(edge):
            at_source = edge // ranks
            other = by_source[at_source * ranks + second]
            by_source[at_source * ranks + second] = edge
            by_source[at_source * ranks + first] = other

            @pl.when(other < 0)
            def _():
                free_source[at_source] = (free_source[at_source] | (1 << first)) & ~(1 << second)

            at_dest = dest_of(table_ref[jnp.maximum(other, 0)])
            following = jnp.where(other < 0, -1, by_dest[at_dest * ranks + first])

            @pl.when(other >= 0)
            def _():
                by_dest[at_dest * ranks + first] = other
                by_dest[at_dest * ranks + second] = following

            @pl.when(jnp.logical_and(other >= 0, following < 0))
            def _():
                free_dest[at_dest] = (free_dest[at_dest] | (1 << second)) & ~(1 << first)

            return following

        lax.while_loop(lambda edge: edge >= 0, swap, moved)
        return carry

    lax.fori_loop(0, ranks * ranks, place, 0)
    for device in range(ranks):
        for k in range(ranks):
            plan_ref[device * ranks + k] = by_source[device * ranks + (device ^ k)]
            plan_ref[(ranks + device) * ranks + k] = by_dest[device * ranks + (device ^ k)]


def plan_routes(table, ranks, dest_of):
    return pl.pallas_call(
        functools.partial(plan_kernel, ranks=ranks, dest_of=dest_of),
        out_shape=jax.ShapeDtypeStruct((2 * ranks * ranks,), jnp.int32),
        in_specs=[pl.BlockSpec(memory_space=pltpu.SMEM)],
        out_specs=pl.BlockSpec(memory_space=pltpu.SMEM),
        scratch_shapes=[pltpu.SMEM((ranks * ranks,), jnp.int32)] * 2 + [pltpu.SMEM((ranks,), jnp.int32)] * 2,
    )(table)


def partial_kernel(
    plan_ref, table_ref, here_ref, act_ref, kv_ref, *rest, ranks, sequence, per_projection, col_blocks, scale
):
    outs, (sums, flipped, sem) = rest[: 2 * ranks], rest[2 * ranks :]
    step = pl.program_id(0)
    blocks, cols_block, rows_block = sums.shape
    group = kv_ref.shape[1] // cols_block

    @pl.when(step == 0)
    def _():
        flipped[...] = kv_ref[...].T

    summed = dot(flipped[...], act_ref[...]) * scale
    sums[pl.ds(step * group, group)] = summed.astype(jnp.bfloat16).reshape(group, cols_block, rows_block)

    @pl.when(step == pl.num_programs(0) - 1)
    def _():
        copies = []
        for k in sequence:
            for relative in [*range(1, ranks, 2), *range(0, ranks, 2)]:
                owner = here_ref[0] ^ relative
                block_id = table_ref[plan_ref[owner * ranks + k]]
                remainder = block_id % per_projection
                index = (
                    remainder // col_blocks * group
                    + block_id // per_projection * col_blocks
                    + remainder % col_blocks
                )
                target = outs[2 * k + 1 - relative % 2].at[relative // 2]
                copy = pltpu.make_async_copy(sums.at[index], target, sem.at[len(copies)])
                copy.start()
                copies.append(copy)
        for copy in copies:
            copy.wait()


def partial_sums(plan, table, here, activations, cotangents, ranks, sequence, rows_block, cols_block, col_blocks):
    tokens, model = activations.shape
    row_blocks = model // rows_block
    blocks = row_blocks * cotangents.shape[1] // cols_block
    body = functools.partial(
        partial_kernel,
        ranks=ranks,
        sequence=sequence,
        per_projection=row_blocks * col_blocks,
        col_blocks=col_blocks,
        scale=1.0 / (tokens * ranks),
    )
    half = jax.ShapeDtypeStruct((ranks // 2, cols_block, rows_block), jnp.bfloat16)
    outs = pl.pallas_call(
        body,
        out_shape=(half,) * (2 * ranks),
        grid_spec=pltpu.PrefetchScalarGridSpec(
            num_scalar_prefetch=3,
            grid=(row_blocks,),
            in_specs=[
                pl.BlockSpec((tokens, rows_block), lambda r, *_: (0, r)),
                pl.BlockSpec(cotangents.shape, lambda r, *_: (0, 0), pipeline_mode=pl.Buffered(1)),
            ],
            out_specs=[pl.BlockSpec(memory_space=pl.ANY)] * (2 * ranks),
            scratch_shapes=[
                pltpu.VMEM((blocks, cols_block, rows_block), jnp.bfloat16),
                pltpu.VMEM(cotangents.shape[::-1], jnp.bfloat16),
                pltpu.SemaphoreType.DMA((ranks * ranks,)),
            ],
        ),
        compiler_params=pltpu.CompilerParams(vmem_limit_bytes=VMEM_LIMIT),
        cost_estimate=pl.CostEstimate(
            flops=2 * activations.size * cotangents.shape[1],
            bytes_accessed=activations.size * 2 + blocks * rows_block * cols_block * 2,
            transcendentals=0,
        ),
    )(plan, table, here, activations, cotangents)
    return [(outs[2 * k], outs[2 * k + 1]) for k in range(ranks)]


def fold_kernel(kept_ref, came_ref, own_ref, *send_refs):
    own_ref[...] = kept_ref[0].astype(jnp.float32) + came_ref[0].astype(jnp.float32)
    for q, send_ref in enumerate(send_refs, 1):
        summed = kept_ref[q].astype(jnp.float32) + came_ref[q].astype(jnp.float32)
        send_ref[...] = summed.astype(jnp.bfloat16)


def fold(kept, came):
    count, cols_block, rows_block = kept.shape
    size = kept.size
    return pl.pallas_call(
        fold_kernel,
        out_shape=(jax.ShapeDtypeStruct((cols_block, rows_block), jnp.float32),)
        + (jax.ShapeDtypeStruct((cols_block, rows_block), jnp.bfloat16),) * (count - 1),
        cost_estimate=pl.CostEstimate(flops=size, bytes_accessed=size * 6, transcendentals=0),
    )(kept, came)


def slot_kernel(plan_ref, here_ref, own_ref, *rest, k, parts, ranks, chained):
    came, rest = rest[:parts], rest[parts:]
    left_ref, right_ref = rest[:2]
    rest = rest[4:] if chained else rest[2:]
    left_out, right_out, dir_ref, left, right, ml, fl, xl, mr, fr, xr, sem = rest
    slot = plan_ref[here_ref[0] * ranks + k] % ranks
    reads = [
        pltpu.make_async_copy(left_ref.at[slot], left, sem.at[0]),
        pltpu.make_async_copy(right_ref.at[slot], right, sem.at[1]),
    ]
    for copy in reads:
        copy.start()
    flipped = own_ref[...]
    for ref in came:
        flipped = flipped + ref[...].astype(jnp.float32)
    grad = flipped.T
    high, low = halves(grad)
    high_t, low_t = halves(flipped)
    wide = jnp.concatenate([high, high, low], axis=1)
    wide_t = jnp.concatenate([high_t, high_t, low_t], axis=1)
    tall = jnp.concatenate([high, low, high], axis=0)
    tall_t = jnp.concatenate([high_t, low_t, high_t], axis=0)
    left_add = (1.0 - MOMENT_DECAY) * dot(wide, tall_t)
    right_add = (1.0 - MOMENT_DECAY) * dot(wide_t, tall)
    for copy in reads:
        copy.wait()
    left_new = MOMENT_DECAY * left[...] + left_add
    right_new = MOMENT_DECAY * right[...] + right_add
    left[...] = left_new
    right[...] = right_new
    writes = [
        pltpu.make_async_copy(left, left_out.at[slot], sem.at[0]),
        pltpu.make_async_copy(right, right_out.at[slot], sem.at[1]),
    ]
    for copy in writes:
        copy.start()
    begin_root(left_new, ml, fl, xl)
    begin_root(right_new, mr, fr, xr)
    groups = [(ml, fl, xl), (mr, fr, xr)]

    def step(_, carry):
        root_steps(groups)
        return carry

    lax.fori_loop(0, ITERS - 1, step, 0)
    root_high, root_low = halves(xl[...])
    half = dot(jnp.concatenate([root_high, root_high, root_low], axis=1), tall)
    half_high, half_low = halves(half)
    right_high, right_low = halves(xr[...])
    precond = dot(
        jnp.concatenate([half_high, half_high, half_low], axis=1),
        jnp.concatenate([right_high, right_low, right_high], axis=0),
    )
    mean = total(precond * precond) / precond.size
    dir_ref[...] = (precond / jnp.sqrt(mean + 1e-06)).astype(jnp.bfloat16)
    for copy in writes:
        copy.wait()


def slot_step(plan, here, own, came, left_factors, right_factors, k, before):
    cols_block, rows_block = own.shape
    ranks = left_factors.shape[0]
    chained = before is not None
    whole = [pl.BlockSpec(own.shape, lambda g, *_: (0, 0))] * (1 + len(came))
    anywhere = pl.BlockSpec(memory_space=pl.ANY)
    operands = [plan, here, own, *came, left_factors, right_factors]
    aliases = {}
    if chained:
        aliases = {len(operands): 0, len(operands) + 1: 1}
        operands += list(before)

    def squares(order):
        square = (order, order)
        return [
            pltpu.VMEM(square, jnp.bfloat16),
            pltpu.VMEM(square, jnp.bfloat16),
            pltpu.VMEM(square, jnp.float32),
        ]

    return pl.pallas_call(
        functools.partial(slot_kernel, k=k, parts=len(came), ranks=ranks, chained=chained),
        out_shape=(
            jax.ShapeDtypeStruct(left_factors.shape, jnp.float32),
            jax.ShapeDtypeStruct(right_factors.shape, jnp.float32),
            jax.ShapeDtypeStruct((rows_block, cols_block), jnp.bfloat16),
        ),
        grid_spec=pltpu.PrefetchScalarGridSpec(
            num_scalar_prefetch=2,
            grid=(1,),
            in_specs=whole + [anywhere] * (4 if chained else 2),
            out_specs=(anywhere, anywhere, pl.BlockSpec((rows_block, cols_block), lambda g, *_: (0, 0))),
            scratch_shapes=[
                pltpu.VMEM((rows_block, rows_block), jnp.float32),
                pltpu.VMEM((cols_block, cols_block), jnp.float32),
                *squares(rows_block),
                *squares(cols_block),
                pltpu.SemaphoreType.DMA((2,)),
            ],
        ),
        input_output_aliases=aliases,
        compiler_params=pltpu.CompilerParams(vmem_limit_bytes=VMEM_LIMIT),
        cost_estimate=pl.CostEstimate(
            flops=2 * rows_block**3 * 4 * ITERS,
            bytes_accessed=rows_block * rows_block * 8,
            transcendentals=0,
        ),
    )(*operands)


def sort_kernel(plan_ref, here_ref, *rest, ranks):
    sources, (out_ref, sem) = rest[:ranks], rest[ranks:]
    for q in range(ranks):
        came_from = plan_ref[(ranks + (here_ref[0] ^ q)) * ranks + q] // ranks ^ here_ref[0]
        for p, source in enumerate(sources):

            @pl.when(came_from == p)
            def _():
                pltpu.make_async_copy(source, out_ref.at[q], sem.at[q]).start()

    for q in range(ranks):
        pltpu.make_async_copy(sources[0], out_ref.at[q], sem.at[q]).wait()


def sort_by_dest(plan, here, directions):
    ranks = len(directions)
    shape = (ranks,) + directions[0].shape
    return pl.pallas_call(
        functools.partial(sort_kernel, ranks=ranks),
        out_shape=jax.ShapeDtypeStruct(shape, jnp.bfloat16),
        grid_spec=pltpu.PrefetchScalarGridSpec(
            num_scalar_prefetch=2,
            grid=(1,),
            in_specs=[pl.BlockSpec(memory_space=pl.ANY)] * ranks,
            out_specs=pl.BlockSpec(shape, lambda g, *_: (0, 0, 0)),
            scratch_shapes=[pltpu.SemaphoreType.DMA((ranks,))],
        ),
    )(plan, here, *directions)


def flip(index, mask):
    bit = 1
    while bit <= mask:
        if mask & bit:
            index = index + bit - index // bit % 2 * (2 * bit)
        bit *= 2
    return index


def exchange_kernel(send_ref, held_ref, dp_send, dp_recv, tp_send, tp_recv, *, ranks, shards):
    me, column = lax.axis_index("dp"), lax.axis_index("tensor")
    bits = [1 << i for i in reversed(range(shards.bit_length() - 1))]
    mesh_id = pl.DeviceIdType.MESH
    barrier = pltpu.get_barrier_semaphore()
    for q in range(1, ranks):
        pl.semaphore_signal(barrier, inc=1, device_id=(flip(me, q), column), device_id_type=mesh_id)
    for bit in bits:
        pl.semaphore_signal(barrier, inc=1, device_id=(me, flip(column, bit)), device_id_type=mesh_id)
    pl.semaphore_wait(barrier, ranks - 1 + len(bits))

    hops = {}
    for q in range(1, ranks):
        hops[q] = pltpu.make_async_remote_copy(
            src_ref=send_ref.at[q],
            dst_ref=held_ref.at[0, q],
            send_sem=dp_send.at[q],
            recv_sem=dp_recv.at[q],
            device_id=(flip(me, q), column),
            device_id_type=mesh_id,
        )
        hops[q].start()
    relays = {}

    def relay(origin, q):
        for bit in bits:
            if origin % (2 * bit) == 0:
                copy = pltpu.make_async_remote_copy(
                    src_ref=send_ref.at[q] if origin == 0 and q == 0 else held_ref.at[origin, q],
                    dst_ref=held_ref.at[origin + bit, q],
                    send_sem=tp_send.at[origin + bit, q],
                    recv_sem=tp_recv.at[origin + bit, q],
                    device_id=(me, flip(column, bit)),
                    device_id_type=mesh_id,
                )
                copy.start()
                relays[origin + bit, q] = copy

    later = [origin for origin in range(1, shards)]
    before = None
    for q in range(ranks):
        if q > 0:
            hops[q].wait_recv()
        relay(0, q)
        if before is not None:
            for origin in later:
                relays[origin, before].wait_recv()
                relay(origin, before)
        before = q
    for origin in later:
        relays[origin, before].wait_recv()
        relay(origin, before)
    for copy in [*hops.values(), *relays.values()]:
        copy.wait_send()


def exchange(sorted_blocks, shards):
    ranks = sorted_blocks.shape[0]
    return pl.pallas_call(
        functools.partial(exchange_kernel, ranks=ranks, shards=shards),
        out_shape=jax.ShapeDtypeStruct((shards,) + sorted_blocks.shape, jnp.bfloat16),
        in_specs=[pl.BlockSpec(memory_space=pltpu.VMEM)],
        out_specs=pl.BlockSpec(memory_space=pl.ANY),
        scratch_shapes=[
            pltpu.SemaphoreType.DMA((ranks,)),
            pltpu.SemaphoreType.DMA((ranks,)),
            pltpu.SemaphoreType.DMA((shards, ranks)),
            pltpu.SemaphoreType.DMA((shards, ranks)),
        ],
        compiler_params=pltpu.CompilerParams(collective_id=0, has_side_effects=True),
    )(sorted_blocks)


def assemble_kernel(plan_ref, table_ref, here_ref, sorted_ref, held_ref, out_ref, sem, *, per_projection, col_blocks):
    shards, ranks, rows_block, cols_block = held_ref.shape
    shard_rows = out_ref.shape[1]
    copies = []
    for q in range(ranks):
        block_id = table_ref[plan_ref[(ranks + here_ref[0]) * ranks + q]]
        remainder = block_id % per_projection
        row_start = pl.multiple_of(remainder // col_blocks * rows_block % shard_rows, rows_block)
        for origin in range(shards):
            shard = here_ref[1] ^ origin
            col_start = pl.multiple_of((shard * col_blocks + remainder % col_blocks) * cols_block, cols_block)
            source = sorted_ref.at[q] if origin == 0 and q == 0 else held_ref.at[origin, q]
            target = out_ref.at[
                block_id // per_projection, pl.ds(row_start, rows_block), pl.ds(col_start, cols_block)
            ]
            copies.append(pltpu.make_async_copy(source, target, sem.at[len(copies)]))
            copies[-1].start()
    for copy in copies:
        copy.wait()


def assemble(plan, table, here, sorted_blocks, held, projections, shard_rows, per_projection, col_blocks):
    shards, ranks, _, cols_block = held.shape
    shape = (projections, shard_rows, shards * col_blocks * cols_block)
    return pl.pallas_call(
        functools.partial(assemble_kernel, per_projection=per_projection, col_blocks=col_blocks),
        out_shape=jax.ShapeDtypeStruct(shape, jnp.bfloat16),
        grid_spec=pltpu.PrefetchScalarGridSpec(
            num_scalar_prefetch=3,
            grid=(1,),
            in_specs=[pl.BlockSpec(memory_space=pl.ANY)] * 2,
            out_specs=pl.BlockSpec(shape, lambda g, *_: (0, 0, 0)),
            scratch_shapes=[pltpu.SemaphoreType.DMA((shards * ranks,))],
        ),
        compiler_params=pltpu.CompilerParams(vmem_limit_bytes=VMEM_LIMIT),
    )(plan, table, here, sorted_blocks, held)


def routed_path(activations, key_value_grads, owner_table, left_factors, right_factors):
    rows_block = left_factors.shape[2]
    cols_block = right_factors.shape[2]
    ranks = lax.axis_size("dp")
    shards = lax.axis_size("tensor")
    projections = key_value_grads.shape[1]
    col_blocks = key_value_grads.shape[2] // cols_block
    per_projection = activations.shape[1] // rows_block * col_blocks
    shard_rows = activations.shape[1] // ranks
    cotangents = key_value_grads.reshape(key_value_grads.shape[0], -1)
    here = jnp.stack([lax.axis_index("dp"), lax.axis_index("tensor")]).astype(jnp.int32)

    def dest_of(block_id):
        return block_id % per_projection // col_blocks * rows_block // shard_rows

    def across(x, mask):
        return lax.ppermute(x, "dp", [(i, i ^ mask) for i in range(ranks)])

    sequence = [*range(1, ranks), 0]
    plan = plan_routes(owner_table, ranks, dest_of)
    halves_of = partial_sums(
        plan, owner_table, here, activations, cotangents, ranks, sequence, rows_block, cols_block, col_blocks
    )
    before = None
    directions = [None] * ranks
    came = {k: across(halves_of[k][0], 1) for k in sequence}
    for k in sequence:
        own, *sends = fold(halves_of[k][1], came[k])
        pieces = [across(send, 2 * q) for q, send in enumerate(sends, 1)]
        left_new, right_new, direction = slot_step(
            plan, here, own, pieces, left_factors[0], right_factors[0], k, before
        )
        before = (left_new, right_new)
        directions[k] = across(direction, k) if k else direction
    sorted_blocks = sort_by_dest(plan, here, directions)
    held = exchange(sorted_blocks, shards)
    update = assemble(
        plan, owner_table, here, sorted_blocks, held, projections, shard_rows, per_projection, col_blocks
    )
    return (left_new[None], right_new[None], update)


def local(activations, key_value_grads, owner_table, left_factors, right_factors):
    ranks, shards = lax.axis_size("dp"), lax.axis_size("tensor")
    shard_rows = activations.shape[1] // ranks
    whole_blocks = shard_rows % left_factors.shape[2] == 0
    powers = ranks & (ranks - 1) == 0 and shards & (shards - 1) == 0
    one_each = left_factors.shape[1] == ranks and ranks > 1
    path = routed_path if whole_blocks and powers and one_each else gathered_path
    return path(activations, key_value_grads, owner_table, left_factors, right_factors)


def solution(mesh):
    in_specs = (
        P("dp", None),
        P("dp", None, "tensor"),
        P(),
        P("tensor", "dp", None, None),
        P("tensor", "dp", None, None),
    )
    out_specs = (P("tensor", "dp", None, None), P("tensor", "dp", None, None), P(None, "dp", None))
    return jax.shard_map(local, mesh=mesh, in_specs=in_specs, out_specs=out_specs, check_vma=False)
```

```python
import functools

import jax
import jax.numpy as jnp
from jax import lax
from jax.experimental import pallas as pl
from jax.experimental.pallas import tpu as pltpu
from jax.sharding import PartitionSpec as P

ITERS = 8
MOMENT_DECAY = 0.9
RIDGE_SHARE = 0.0001
CHUNK_SLOTS = 2
VMEM_LIMIT = 60 * 1024 * 1024


def dot(left_mat, right_mat):
    return jnp.dot(left_mat, right_mat, preferred_element_type=jnp.float32)


def halves(x):
    high = x.astype(jnp.bfloat16)
    low = (x - high.astype(jnp.float32)).astype(jnp.bfloat16)
    return high, low


def gradient_kernel(
    table_ref, act_ref, kv_ref, out_ref, *, chunk, chunk_slots, slots, per_projection, col_blocks, scale
):
    rows_block, cols_block = out_ref.shape[2:]
    width = col_blocks * cols_block
    first = pl.program_id(0) * slots + chunk * chunk_slots
    for k in range(chunk_slots):
        block_id = table_ref[first + k]
        projection = block_id // per_projection
        remainder = block_id % per_projection
        row_start = pl.multiple_of(remainder // col_blocks * rows_block, rows_block)
        col_start = pl.multiple_of(
            projection * width + remainder % col_blocks * cols_block, cols_block
        )
        summed = lax.dot_general(
            act_ref[:, pl.ds(row_start, rows_block)],
            kv_ref[:, pl.ds(col_start, cols_block)],
            (((0,), (0,)), ((), ())),
            preferred_element_type=jnp.float32,
        )
        out_ref[0, k] = summed * scale


def gradient_chunk(table, activations, cotangents, chunk, chunk_slots, ranks, rows_block, cols_block, col_blocks):
    tokens, model = activations.shape
    slots = table.shape[0] // ranks
    body = functools.partial(
        gradient_kernel,
        chunk=chunk,
        chunk_slots=chunk_slots,
        slots=slots,
        per_projection=model // rows_block * col_blocks,
        col_blocks=col_blocks,
        scale=1.0 / (tokens * ranks),
    )
    return pl.pallas_call(
        body,
        out_shape=jax.ShapeDtypeStruct((ranks, chunk_slots, rows_block, cols_block), jnp.float32),
        grid_spec=pltpu.PrefetchScalarGridSpec(
            num_scalar_prefetch=1,
            grid=(ranks,),
            in_specs=[
                pl.BlockSpec(activations.shape, lambda d, t: (0, 0), pipeline_mode=pl.Buffered(1)),
                pl.BlockSpec(cotangents.shape, lambda d, t: (0, 0), pipeline_mode=pl.Buffered(1)),
            ],
            out_specs=pl.BlockSpec(
                (1, chunk_slots, rows_block, cols_block), lambda d, t: (d, 0, 0, 0)
            ),
        ),
        compiler_params=pltpu.CompilerParams(vmem_limit_bytes=VMEM_LIMIT),
        cost_estimate=pl.CostEstimate(
            flops=2 * ranks * chunk_slots * rows_block * cols_block * tokens,
            bytes_accessed=activations.size * 2 + ranks * chunk_slots * rows_block * cols_block * 4,
            transcendentals=0,
        ),
    )(table, activations, cotangents)


def diagonal(order):
    rows = lax.broadcasted_iota(jnp.int32, (order, order), 0)
    return rows == lax.broadcasted_iota(jnp.int32, (order, order), 1)


def total(x):
    return jnp.sum(jnp.sum(x, axis=1, keepdims=True), axis=0, keepdims=True)


def factor_of(powered, on_diagonal):
    return ((jnp.where(on_diagonal, 5.0, 0.0) - powered) * 0.25).astype(jnp.bfloat16)


def begin_root(updated, m_ref, f_ref, x_ref):
    order = updated.shape[0]
    on_diagonal = diagonal(order)
    trace = total(jnp.where(on_diagonal, updated, 0.0))
    shifted = updated + jnp.where(on_diagonal, RIDGE_SHARE * trace / order, 0.0)
    scaling = 2.5 / jnp.sqrt(total(shifted * shifted))
    powered = scaling * shifted
    factor = factor_of(powered, on_diagonal)
    start = jnp.sqrt(jnp.sqrt(scaling)).astype(jnp.bfloat16).astype(jnp.float32)
    m_ref[...] = powered.astype(jnp.bfloat16)
    f_ref[...] = factor
    x_ref[...] = start * factor.astype(jnp.float32)


def root_steps(groups):
    squares = []
    for m_ref, f_ref, x_ref in groups:
        factor = f_ref[...]
        squares.append(dot(factor, factor).astype(jnp.bfloat16))
    fourths = [dot(s, s).astype(jnp.bfloat16) for s in squares]
    for fourth, (m_ref, f_ref, x_ref) in zip(fourths, groups):
        powered = dot(fourth, m_ref[...])
        m_ref[...] = powered.astype(jnp.bfloat16)
        f_ref[...] = factor_of(powered, diagonal(powered.shape[0]))
    for m_ref, f_ref, x_ref in groups:
        x_ref[...] = dot(x_ref[...].astype(jnp.bfloat16), f_ref[...])


def block_kernel(grad_ref, left_ref, right_ref, *rest, chunk_slots, chained):
    if chained:
        rest = rest[2:]
    left_out, right_out, dir_ref, ml, fl, xl, mr, fr, xr = rest
    groups = []
    for k in range(chunk_slots):
        grad = grad_ref[k]
        high, low = halves(grad)
        flipped = grad.T
        high_t, low_t = halves(flipped)
        wide = jnp.concatenate([high, high, low], axis=1)
        wide_t = jnp.concatenate([high_t, high_t, low_t], axis=1)
        tall = jnp.concatenate([high, low, high], axis=0)
        tall_t = jnp.concatenate([high_t, low_t, high_t], axis=0)
        left_new = MOMENT_DECAY * left_ref[k] + (1.0 - MOMENT_DECAY) * dot(wide, tall_t)
        right_new = MOMENT_DECAY * right_ref[k] + (1.0 - MOMENT_DECAY) * dot(wide_t, tall)
        left_out[k] = left_new
        right_out[k] = right_new
        begin_root(left_new, ml.at[k], fl.at[k], xl.at[k])
        begin_root(right_new, mr.at[k], fr.at[k], xr.at[k])
        groups.append((ml.at[k], fl.at[k], xl.at[k]))
        groups.append((mr.at[k], fr.at[k], xr.at[k]))

    def step(_, carry):
        root_steps(groups)
        return carry

    lax.fori_loop(0, ITERS - 1, step, 0)
    for k in range(chunk_slots):
        high, low = halves(grad_ref[k])
        tall = jnp.concatenate([high, low, high], axis=0)
        root_high, root_low = halves(xl[k])
        half = dot(jnp.concatenate([root_high, root_high, root_low], axis=1), tall)
        half_high, half_low = halves(half)
        right_high, right_low = halves(xr[k])
        precond = dot(
            jnp.concatenate([half_high, half_high, half_low], axis=1),
            jnp.concatenate([right_high, right_low, right_high], axis=0),
        )
        mean = total(precond * precond) / precond.size
        dir_ref[k] = (precond / jnp.sqrt(mean + 1e-06)).astype(jnp.bfloat16)


def block_chunk(grads, left_factors, right_factors, chunk, before):
    chunk_slots, rows_block, cols_block = grads.shape

    def pick(*tail):
        return pl.BlockSpec((chunk_slots,) + tail, lambda g: (chunk, 0, 0))

    def whole(*tail):
        return pl.BlockSpec((chunk_slots,) + tail, lambda g: (0, 0, 0))

    chained = before is not None
    specs = [
        whole(rows_block, cols_block),
        pick(rows_block, rows_block),
        pick(cols_block, cols_block),
    ]
    operands = [grads, left_factors, right_factors]
    aliases = {}
    if chained:
        specs += [pl.BlockSpec(memory_space=pl.ANY)] * 2
        operands += list(before)
        aliases = {3: 0, 4: 1}

    def scratch(order):
        square = (chunk_slots, order, order)
        return [
            pltpu.VMEM(square, jnp.bfloat16),
            pltpu.VMEM(square, jnp.bfloat16),
            pltpu.VMEM(square, jnp.float32),
        ]

    return pl.pallas_call(
        functools.partial(block_kernel, chunk_slots=chunk_slots, chained=chained),
        grid=(1,),
        out_shape=(
            jax.ShapeDtypeStruct(left_factors.shape, jnp.float32),
            jax.ShapeDtypeStruct(right_factors.shape, jnp.float32),
            jax.ShapeDtypeStruct(grads.shape, jnp.bfloat16),
        ),
        in_specs=specs,
        out_specs=(
            pick(rows_block, rows_block),
            pick(cols_block, cols_block),
            whole(rows_block, cols_block),
        ),
        scratch_shapes=scratch(rows_block) + scratch(cols_block),
        input_output_aliases=aliases,
        compiler_params=pltpu.CompilerParams(vmem_limit_bytes=VMEM_LIMIT),
        cost_estimate=pl.CostEstimate(
            flops=2 * chunk_slots * rows_block**3 * 4 * ITERS,
            bytes_accessed=chunk_slots * rows_block * rows_block * 8,
            transcendentals=0,
        ),
    )(*operands)


def pick_kernel(dev_ref, pos_ref, sub_ref, *refs, shape, chunk_slots, piece_rows, cols_block):
    sources, out_ref, sem = refs[:-2], refs[-2], refs[-1]
    projections, per_shard, col_blocks = shape
    index = 0
    for projection in range(projections):
        for piece in range(per_shard):
            for column in range(col_blocks):
                dest = out_ref.at[
                    projection,
                    pl.ds(piece * piece_rows, piece_rows),
                    pl.ds(column * cols_block, cols_block),
                ]
                rows = pl.ds(pl.multiple_of(sub_ref[piece] * piece_rows, piece_rows), piece_rows)
                for chunk, source in enumerate(sources):

                    @pl.when(pos_ref[index] // chunk_slots == chunk)
                    def _():
                        pltpu.make_async_copy(
                            source.at[dev_ref[index], pos_ref[index] % chunk_slots, rows], dest, sem.at[index]
                        ).start()

                index += 1
    index = 0
    for projection in range(projections):
        for piece in range(per_shard):
            for column in range(col_blocks):
                dest = out_ref.at[
                    projection,
                    pl.ds(piece * piece_rows, piece_rows),
                    pl.ds(column * cols_block, cols_block),
                ]
                pltpu.make_async_copy(
                    sources[0].at[0, 0, pl.ds(0, piece_rows)], dest, sem.at[index]
                ).wait()
                index += 1


def pick_rows(gathered, owner_table, shard_rows, row_blocks, col_blocks, slots):
    _, chunk_slots, block_order, cols_block = gathered[0].shape
    piece_rows = min(shard_rows, block_order)
    per_block = block_order // piece_rows
    per_shard = shard_rows // piece_rows
    pieces = lax.axis_index("dp") * per_shard + jnp.arange(per_shard, dtype=jnp.int32)
    wanted = (
        jnp.arange(2, dtype=jnp.int32)[:, None, None] * row_blocks + (pieces // per_block)[None, :, None]
    ) * col_blocks + jnp.arange(col_blocks, dtype=jnp.int32)[None, None, :]
    hits = wanted.reshape(-1)[:, None] == owner_table[None, :]
    where = jnp.sum(
        jnp.where(hits, jnp.arange(owner_table.shape[0], dtype=jnp.int32)[None, :], 0), axis=1, dtype=jnp.int32
    )
    count = 2 * per_shard * col_blocks
    body = functools.partial(
        pick_kernel,
        shape=(2, per_shard, col_blocks),
        chunk_slots=chunk_slots,
        piece_rows=piece_rows,
        cols_block=cols_block,
    )
    shape = (2, shard_rows, col_blocks * cols_block)
    return pl.pallas_call(
        body,
        out_shape=jax.ShapeDtypeStruct(shape, jnp.bfloat16),
        grid_spec=pltpu.PrefetchScalarGridSpec(
            num_scalar_prefetch=3,
            grid=(1,),
            in_specs=[pl.BlockSpec(memory_space=pl.ANY)] * len(gathered),
            out_specs=pl.BlockSpec(shape, lambda g, *_: (0, 0, 0)),
            scratch_shapes=[pltpu.SemaphoreType.DMA((count,))],
        ),
    )(where // slots, where % slots, pieces % per_block, *gathered)


def gathered_path(activations, key_value_grads, owner_table, left_factors, right_factors):
    rows_block = left_factors.shape[2]
    cols_block = right_factors.shape[2]
    ranks = lax.axis_size("dp")
    row_blocks = activations.shape[1] // rows_block
    col_blocks = key_value_grads.shape[2] // cols_block
    shard_rows = activations.shape[1] // ranks
    slots = left_factors.shape[1]
    chunk_slots = min(CHUNK_SLOTS, slots)
    cotangents = key_value_grads.reshape(key_value_grads.shape[0], -1)
    grads = []
    for chunk in range(slots // chunk_slots):
        partial = gradient_chunk(
            owner_table, activations, cotangents, chunk, chunk_slots, ranks, rows_block, cols_block, col_blocks
        )
        grads.append(lax.psum_scatter(partial, "dp", scatter_dimension=0, tiled=True)[0])
    before = None
    gathered = []
    for chunk, grad in enumerate(grads):
        left_new, right_new, directions = block_chunk(grad, left_factors[0], right_factors[0], chunk, before)
        before = (left_new, right_new)
        gathered.append(lax.all_gather(directions, "dp", axis=0))
    own_rows = pick_rows(gathered, owner_table, shard_rows, row_blocks, col_blocks, slots)
    update = lax.all_gather(own_rows, "tensor", axis=2, tiled=True)
    return (left_new[None], right_new[None], update)


def plan_kernel(table_ref, plan_ref, by_source, by_dest, free_source, free_dest, *, ranks, dest_of):
    def lowest(mask):
        found = 0
        for colour in reversed(range(ranks)):
            found = jnp.where((mask >> colour) & 1 == 1, colour, found)
        return found

    def clear(i, carry):
        by_source[i] = -1
        by_dest[i] = -1
        return carry

    lax.fori_loop(0, ranks * ranks, clear, 0)
    for i in range(ranks):
        free_source[i] = (1 << ranks) - 1
        free_dest[i] = (1 << ranks) - 1

    def place(slot, carry):
        source = slot // ranks
        dest = dest_of(table_ref[slot])
        both = free_source[source] & free_dest[dest]
        shared = both != 0
        first = lowest(jnp.where(shared, both, free_source[source]))
        second = lowest(jnp.where(shared, both, free_dest[dest]))
        moved = by_dest[dest * ranks + first]
        by_dest[dest * ranks + first] = slot
        by_source[source * ranks + first] = slot
        free_source[source] = free_source[source] & ~(1 << first)
        free_dest[dest] = free_dest[dest] & ~(1 << second)

        @pl.when(jnp.logical_not(shared))
        def _():
            by_dest[dest * ranks + second] = moved

        def swap(edge):
            at_source = edge // ranks
            other = by_source[at_source * ranks + second]
            by_source[at_source * ranks + second] = edge
            by_source[at_source * ranks + first] = other

            @pl.when(other < 0)
            def _():
                free_source[at_source] = (free_source[at_source] | (1 << first)) & ~(1 << second)

            at_dest = dest_of(table_ref[jnp.maximum(other, 0)])
            following = jnp.where(other < 0, -1, by_dest[at_dest * ranks + first])

            @pl.when(other >= 0)
            def _():
                by_dest[at_dest * ranks + first] = other
                by_dest[at_dest * ranks + second] = following

            @pl.when(jnp.logical_and(other >= 0, following < 0))
            def _():
                free_dest[at_dest] = (free_dest[at_dest] | (1 << second)) & ~(1 << first)

            return following

        lax.while_loop(lambda edge: edge >= 0, swap, moved)
        return carry

    lax.fori_loop(0, ranks * ranks, place, 0)
    for device in range(ranks):
        for k in range(ranks):
            plan_ref[device * ranks + k] = by_source[device * ranks + (device ^ k)]
            plan_ref[(ranks + device) * ranks + k] = by_dest[device * ranks + (device ^ k)]


def plan_routes(table, ranks, dest_of):
    return pl.pallas_call(
        functools.partial(plan_kernel, ranks=ranks, dest_of=dest_of),
        out_shape=jax.ShapeDtypeStruct((2 * ranks * ranks,), jnp.int32),
        in_specs=[pl.BlockSpec(memory_space=pltpu.SMEM)],
        out_specs=pl.BlockSpec(memory_space=pltpu.SMEM),
        scratch_shapes=[pltpu.SMEM((ranks * ranks,), jnp.int32)] * 2 + [pltpu.SMEM((ranks,), jnp.int32)] * 2,
    )(table)


def partial_kernel(
    plan_ref, table_ref, here_ref, act_ref, kv_ref, send_ref, kept_ref, sums, flipped, sem, *, ranks, per_projection, col_blocks, scale
):
    step = pl.program_id(0)
    blocks, cols_block, rows_block = sums.shape
    group = kv_ref.shape[1] // cols_block

    @pl.when(step == 0)
    def _():
        flipped[...] = kv_ref[...].T

    summed = dot(flipped[...], act_ref[...]) * scale
    sums[pl.ds(step * group, group)] = summed.astype(jnp.bfloat16).reshape(group, cols_block, rows_block)

    @pl.when(step == pl.num_programs(0) - 1)
    def _():
        copies = []
        for i in range(ranks):
            for relative in [*range(1, ranks, 2), *range(0, ranks, 2)]:
                owner = here_ref[0] ^ relative
                block_id = table_ref[plan_ref[owner * ranks + (i + 1) % ranks]]
                remainder = block_id % per_projection
                index = (
                    remainder // col_blocks * group
                    + block_id // per_projection * col_blocks
                    + remainder % col_blocks
                )
                target = (send_ref if relative % 2 else kept_ref).at[i, relative // 2]
                copy = pltpu.make_async_copy(sums.at[index], target, sem.at[len(copies)])
                copy.start()
                copies.append(copy)
        for copy in copies:
            copy.wait()


def partial_sums(plan, table, here, activations, cotangents, ranks, rows_block, cols_block, col_blocks):
    tokens, model = activations.shape
    row_blocks = model // rows_block
    blocks = row_blocks * cotangents.shape[1] // cols_block
    body = functools.partial(
        partial_kernel,
        ranks=ranks,
        per_projection=row_blocks * col_blocks,
        col_blocks=col_blocks,
        scale=1.0 / (tokens * ranks),
    )
    half = jax.ShapeDtypeStruct((ranks, ranks // 2, cols_block, rows_block), jnp.bfloat16)
    return pl.pallas_call(
        body,
        out_shape=(half, half),
        grid_spec=pltpu.PrefetchScalarGridSpec(
            num_scalar_prefetch=3,
            grid=(row_blocks,),
            in_specs=[
                pl.BlockSpec((tokens, rows_block), lambda r, *_: (0, r)),
                pl.BlockSpec(cotangents.shape, lambda r, *_: (0, 0), pipeline_mode=pl.Buffered(1)),
            ],
            out_specs=[pl.BlockSpec(memory_space=pl.ANY)] * 2,
            scratch_shapes=[
                pltpu.VMEM((blocks, cols_block, rows_block), jnp.bfloat16),
                pltpu.VMEM(cotangents.shape[::-1], jnp.bfloat16),
                pltpu.SemaphoreType.DMA((ranks * ranks,)),
            ],
        ),
        compiler_params=pltpu.CompilerParams(vmem_limit_bytes=VMEM_LIMIT),
    )(plan, table, here, activations, cotangents)


def flip(index, mask, size):
    flipped, bit = 0, 1
    while bit < size:
        flipped = flipped + (index // bit + mask // bit) % 2 * bit
        bit *= 2
    return flipped


def main_kernel(
    plan_ref, send_ref, kept_ref, left_ref, right_ref, left_out, right_out, held_ref,
    lefts, rights, left_stage, right_stage, kept, came_y, own, send_z, came_z, ways, arrived, ordered,
    ml, fl, xl, mr, fr, xr,
    load_sem, out_sem, local_sem, y_send, y_recv, z_send, z_recv, way_send, way_recv, dp_send, dp_recv, tp_send, tp_recv,
    *, ranks, shards, pair,
):
    me, column = lax.axis_index("dp"), lax.axis_index("tensor")
    mesh_id = pl.DeviceIdType.MESH
    half = ranks // 2
    bits = [1 << i for i in reversed(range(shards.bit_length() - 1))]

    loads = []
    for i in range(ranks):
        loads.append(pltpu.make_async_copy(kept_ref.at[i], kept.at[i], load_sem.at[0, i]))
        loads.append(pltpu.make_async_copy(left_ref.at[i], lefts.at[i], load_sem.at[1, i]))
        loads.append(pltpu.make_async_copy(right_ref.at[i], rights.at[i], load_sem.at[2, i]))
    for copy in loads:
        copy.start()

    barrier = pltpu.get_barrier_semaphore()
    for q in range(1, ranks):
        pl.semaphore_signal(barrier, inc=1, device_id=(flip(me, q, ranks), column), device_id_type=mesh_id)
    for bit in bits:
        pl.semaphore_signal(barrier, inc=1, device_id=(me, flip(column, bit, shards)), device_id_type=mesh_id)
    pl.semaphore_wait(barrier, ranks - 1 + len(bits))

    def along_dp(source, target, sent, received, mask):
        return pltpu.make_async_remote_copy(
            src_ref=source,
            dst_ref=target,
            send_sem=sent,
            recv_sem=received,
            device_id=(flip(me, mask, ranks), column),
            device_id_type=mesh_id,
        )

    def first_hop(i):
        return along_dp(send_ref.at[i], came_y.at[i], y_send.at[i], y_recv.at[i], 1)

    def second_hop(i, q):
        return along_dp(send_z.at[i, q - 1], came_z.at[i, q - 1], z_send.at[i, q - 1], z_recv.at[i, q - 1], 2 * q)

    def way(i):
        k = (i + 1) % ranks
        return along_dp(ways.at[i], arrived.at[i], way_send.at[i], way_recv.at[i], k)

    for i in range(ranks):
        first_hop(i).start()
    for copy in loads:
        copy.wait()

    def fold(i):
        first_hop(i).wait_recv()
        own[i] = kept[i, 0].astype(jnp.float32) + came_y[i, 0].astype(jnp.float32)
        for q in range(1, half):
            summed = kept[i, q].astype(jnp.float32) + came_y[i, q].astype(jnp.float32)
            send_z[i, q - 1] = summed.astype(jnp.bfloat16)

    def send(i):
        for q in range(1, half):
            second_hop(i, q).start()

    for i in range(pair):
        fold(i)
    for i in range(pair):
        send(i)

    def outs(p):
        copies = []
        for k in range(pair):
            i = p * pair + k
            copies.append(pltpu.make_async_copy(left_stage.at[k], left_out.at[i], out_sem.at[0, k]))
            copies.append(pltpu.make_async_copy(right_stage.at[k], right_out.at[i], out_sem.at[1, k]))
        return copies

    def group(p, more):
        if more:
            fold((p + 1) * pair)
            send((p + 1) * pair)
        groups = []
        for k in range(pair):
            i = p * pair + k
            slot = plan_ref[me * ranks + (i + 1) % ranks] % ranks
            for q in range(1, half):
                second_hop(i, q).wait_recv()
            flipped = own[i]
            for q in range(1, half):
                flipped = flipped + came_z[i, q - 1].astype(jnp.float32)
            own[i] = flipped
            grad = flipped.T
            high, low = halves(grad)
            high_t, low_t = halves(flipped)
            wide = jnp.concatenate([high, high, low], axis=1)
            wide_t = jnp.concatenate([high_t, high_t, low_t], axis=1)
            tall = jnp.concatenate([high, low, high], axis=0)
            tall_t = jnp.concatenate([high_t, low_t, high_t], axis=0)
            left_new = MOMENT_DECAY * lefts[slot] + (1.0 - MOMENT_DECAY) * dot(wide, tall_t)
            right_new = MOMENT_DECAY * rights[slot] + (1.0 - MOMENT_DECAY) * dot(wide_t, tall)
            left_stage[k] = left_new
            right_stage[k] = right_new
            begin_root(left_new, ml.at[k], fl.at[k], xl.at[k])
            begin_root(right_new, mr.at[k], fr.at[k], xr.at[k])
            groups.append((ml.at[k], fl.at[k], xl.at[k]))
            groups.append((mr.at[k], fr.at[k], xr.at[k]))
        for copy in outs(p):
            copy.start()

        def step(_, carry):
            root_steps(groups)
            return carry

        lax.fori_loop(0, (ITERS - 1) // 2, step, 0)
        for k in range(1, pair if more else 1):
            fold((p + 1) * pair + k)
            send((p + 1) * pair + k)
        lax.fori_loop((ITERS - 1) // 2, ITERS - 1, step, 0)
        for k in range(pair):
            i = p * pair + k
            high, low = halves(own[i].T)
            tall = jnp.concatenate([high, low, high], axis=0)
            root_high, root_low = halves(xl[k])
            half_pre = dot(jnp.concatenate([root_high, root_high, root_low], axis=1), tall)
            half_high, half_low = halves(half_pre)
            right_high, right_low = halves(xr[k])
            precond = dot(
                jnp.concatenate([half_high, half_high, half_low], axis=1),
                jnp.concatenate([right_high, right_low, right_high], axis=0),
            )
            mean = total(precond * precond) / precond.size
            ways[i] = (precond / jnp.sqrt(mean + 1e-06)).astype(jnp.bfloat16)
        for copy in outs(p):
            copy.wait()
        for k in range(pair if more else pair - 1):
            way(p * pair + k).start()

    def grouped(p, carry):
        group(p, True)
        return carry

    last = ranks // pair - 1
    lax.fori_loop(0, last, grouped, 0)
    group(last, False)
    arrived[ranks - 1] = ways[ranks - 1]
    for i in range(ranks - 1):
        way(i).wait_recv()

    hops, relays = {}, {}
    for q in [*range(1, ranks), 0]:
        came_from = flip(plan_ref[(ranks + flip(me, q, ranks)) * ranks + q] // ranks, me, ranks)
        ordered[q] = arrived[(came_from + ranks - 1) % ranks]
        if q > 0:
            hops[q] = along_dp(ordered.at[q], held_ref.at[0, q], dp_send.at[q], dp_recv.at[q], q)
            hops[q].start()
    mine = pltpu.make_async_copy(ordered.at[0], held_ref.at[0, 0], local_sem)
    mine.start()

    def relay(origin, q):
        for bit in bits:
            if origin % (2 * bit) == 0:
                copy = pltpu.make_async_remote_copy(
                    src_ref=ordered.at[q] if origin == 0 and q == 0 else held_ref.at[origin, q],
                    dst_ref=held_ref.at[origin + bit, q],
                    send_sem=tp_send.at[origin + bit, q],
                    recv_sem=tp_recv.at[origin + bit, q],
                    device_id=(me, flip(column, bit, shards)),
                    device_id_type=mesh_id,
                )
                copy.start()
                relays[origin + bit, q] = copy

    before = None
    for q in range(ranks):
        if q > 0:
            hops[q].wait_recv()
        relay(0, q)
        if before is not None:
            for origin in range(1, shards):
                relays[origin, before].wait_recv()
                relay(origin, before)
        before = q
    for origin in range(1, shards):
        relays[origin, before].wait_recv()
        relay(origin, before)
    mine.wait()
    for i in range(ranks):
        first_hop(i).wait_send()
        for q in range(1, half):
            second_hop(i, q).wait_send()
        if i < ranks - 1:
            way(i).wait_send()
    for copy in [*hops.values(), *relays.values()]:
        copy.wait_send()


def main_step(plan, sends, kept, left_factors, right_factors, shards):
    ranks, half, cols_block, rows_block = sends.shape
    pair = CHUNK_SLOTS
    f32, bf16 = jnp.float32, jnp.bfloat16
    anywhere = pl.BlockSpec(memory_space=pl.ANY)

    def squares(order):
        square = (pair, order, order)
        return [pltpu.VMEM(square, bf16), pltpu.VMEM(square, bf16), pltpu.VMEM(square, f32)]

    flat, tall = (cols_block, rows_block), (rows_block, cols_block)
    dma = pltpu.SemaphoreType.DMA
    return pl.pallas_call(
        functools.partial(main_kernel, ranks=ranks, shards=shards, pair=pair),
        out_shape=(
            jax.ShapeDtypeStruct(left_factors.shape, f32),
            jax.ShapeDtypeStruct(right_factors.shape, f32),
            jax.ShapeDtypeStruct((shards, ranks) + tall, bf16),
        ),
        in_specs=[pl.BlockSpec(memory_space=pltpu.SMEM)] + [anywhere] * 4,
        out_specs=(anywhere,) * 3,
        scratch_shapes=[
            pltpu.VMEM(left_factors.shape, f32),
            pltpu.VMEM(right_factors.shape, f32),
            pltpu.VMEM((pair,) + left_factors.shape[1:], f32),
            pltpu.VMEM((pair,) + right_factors.shape[1:], f32),
            pltpu.VMEM((ranks, half) + flat, bf16),
            pltpu.VMEM((ranks, half) + flat, bf16),
            pltpu.VMEM((ranks,) + flat, f32),
            pltpu.VMEM((ranks, half - 1) + flat, bf16),
            pltpu.VMEM((ranks, half - 1) + flat, bf16),
            pltpu.VMEM((ranks,) + tall, bf16),
            pltpu.VMEM((ranks,) + tall, bf16),
            pltpu.VMEM((ranks,) + tall, bf16),
            *squares(rows_block),
            *squares(cols_block),
            dma((3, ranks)),
            dma((2, pair)),
            dma,
            dma((ranks,)),
            dma((ranks,)),
            dma((ranks, half - 1)),
            dma((ranks, half - 1)),
            dma((ranks,)),
            dma((ranks,)),
            dma((ranks,)),
            dma((ranks,)),
            dma((shards, ranks)),
            dma((shards, ranks)),
        ],
        compiler_params=pltpu.CompilerParams(
            collective_id=0, has_side_effects=True, vmem_limit_bytes=VMEM_LIMIT
        ),
    )(plan, sends, kept, left_factors, right_factors)


def place_kernel(plan_ref, here_ref, left_ref, right_ref, left_out, right_out):
    left_out[...] = left_ref[...]
    right_out[...] = right_ref[...]


def place_slots(plan, here, left_new, right_new):
    ranks = left_new.shape[0]

    def slot_of(i, plan_ref, here_ref):
        return (plan_ref[here_ref[0] * ranks + (i + 1) % ranks] % ranks, 0, 0)

    def block(x):
        return (1,) + x.shape[1:]

    return pl.pallas_call(
        place_kernel,
        out_shape=(
            jax.ShapeDtypeStruct(left_new.shape, jnp.float32),
            jax.ShapeDtypeStruct(right_new.shape, jnp.float32),
        ),
        grid_spec=pltpu.PrefetchScalarGridSpec(
            num_scalar_prefetch=2,
            grid=(ranks,),
            in_specs=[
                pl.BlockSpec(block(left_new), lambda i, *_: (i, 0, 0)),
                pl.BlockSpec(block(right_new), lambda i, *_: (i, 0, 0)),
            ],
            out_specs=(pl.BlockSpec(block(left_new), slot_of), pl.BlockSpec(block(right_new), slot_of)),
        ),
    )(plan, here, left_new, right_new)


def assemble_kernel(plan_ref, table_ref, here_ref, held_ref, out_ref, sem, *, per_projection, col_blocks):
    shards, ranks, rows_block, cols_block = held_ref.shape
    shard_rows = out_ref.shape[1]
    copies = []
    for q in range(ranks):
        block_id = table_ref[plan_ref[(ranks + here_ref[0]) * ranks + q]]
        remainder = block_id % per_projection
        row_start = pl.multiple_of(remainder // col_blocks * rows_block % shard_rows, rows_block)
        for origin in range(shards):
            shard = here_ref[1] ^ origin
            col_start = pl.multiple_of((shard * col_blocks + remainder % col_blocks) * cols_block, cols_block)
            source = held_ref.at[origin, q]
            target = out_ref.at[
                block_id // per_projection, pl.ds(row_start, rows_block), pl.ds(col_start, cols_block)
            ]
            copies.append(pltpu.make_async_copy(source, target, sem.at[len(copies)]))
            copies[-1].start()
    for copy in copies:
        copy.wait()


def assemble(plan, table, here, held, projections, shard_rows, per_projection, col_blocks):
    shards, ranks, _, cols_block = held.shape
    shape = (projections, shard_rows, shards * col_blocks * cols_block)
    return pl.pallas_call(
        functools.partial(assemble_kernel, per_projection=per_projection, col_blocks=col_blocks),
        out_shape=jax.ShapeDtypeStruct(shape, jnp.bfloat16),
        grid_spec=pltpu.PrefetchScalarGridSpec(
            num_scalar_prefetch=3,
            grid=(1,),
            in_specs=[pl.BlockSpec(memory_space=pl.ANY)],
            out_specs=pl.BlockSpec(shape, lambda g, *_: (0, 0, 0)),
            scratch_shapes=[pltpu.SemaphoreType.DMA((shards * ranks,))],
        ),
        compiler_params=pltpu.CompilerParams(vmem_limit_bytes=VMEM_LIMIT),
    )(plan, table, here, held)


def routed_path(activations, key_value_grads, owner_table, left_factors, right_factors):
    rows_block = left_factors.shape[2]
    cols_block = right_factors.shape[2]
    ranks = lax.axis_size("dp")
    shards = lax.axis_size("tensor")
    projections = key_value_grads.shape[1]
    col_blocks = key_value_grads.shape[2] // cols_block
    per_projection = activations.shape[1] // rows_block * col_blocks
    shard_rows = activations.shape[1] // ranks
    cotangents = key_value_grads.reshape(key_value_grads.shape[0], -1)
    here = jnp.stack([lax.axis_index("dp"), lax.axis_index("tensor")]).astype(jnp.int32)

    def dest_of(block_id):
        return block_id % per_projection // col_blocks * rows_block // shard_rows

    plan = plan_routes(owner_table, ranks, dest_of)
    sends, kept = partial_sums(
        plan, owner_table, here, activations, cotangents, ranks, rows_block, cols_block, col_blocks
    )
    left_new, right_new, held = main_step(plan, sends, kept, left_factors[0], right_factors[0], shards)
    left_new, right_new = place_slots(plan, here, left_new, right_new)
    update = assemble(plan, owner_table, here, held, projections, shard_rows, per_projection, col_blocks)
    return (left_new[None], right_new[None], update)


def local(activations, key_value_grads, owner_table, left_factors, right_factors):
    ranks, shards = lax.axis_size("dp"), lax.axis_size("tensor")
    shard_rows = activations.shape[1] // ranks
    whole_blocks = shard_rows % left_factors.shape[2] == 0
    powers = ranks & (ranks - 1) == 0 and shards & (shards - 1) == 0
    one_each = left_factors.shape[1] == ranks and ranks % CHUNK_SLOTS == 0
    path = routed_path if whole_blocks and powers and one_each else gathered_path
    return path(activations, key_value_grads, owner_table, left_factors, right_factors)


def solution(mesh):
    in_specs = (
        P("dp", None),
        P("dp", None, "tensor"),
        P(),
        P("tensor", "dp", None, None),
        P("tensor", "dp", None, None),
    )
    out_specs = (P("tensor", "dp", None, None), P("tensor", "dp", None, None), P(None, "dp", None))
    return jax.shard_map(local, mesh=mesh, in_specs=in_specs, out_specs=out_specs, check_vma=False)
```
